32 devices in a mesh: groups: 2 (over y), blk: 4 (over z), feat: 2 (over x), sub: 2 (over core).
Axes of the slice: x: 2, y: 2, z: 4, core: 2. Of those that a mesh axis runs over, the one named last changes fastest.
Arguments:
- frames: bfloat16 [16384, 1024], P(('groups', 'blk', 'sub'), 'feat'), parts along dimension 0, may hold values from -6 to 6
- clip_label: int32 [16384], P(('groups', 'blk', 'sub')), parts along dimension 0, may hold values from 0 to 8191, as said below
Outputs:
- duplicate_score: float32 [16384], P(('groups', 'blk', 'sub')), parts along dimension 0
The draws below stay inside these ranges and needn't reach their ends.
There are 2 independent parts, one for each index of `groups`. The reference program is written for one: setup_inputs(seed, part) draws one part's arguments, and reference() takes and returns one part's arrays. A program takes and returns all parts, laid end to end along the dimension named above; each array names one. Nothing has to cross between parts.
Inputs may be any that keep to these rules, and one draw needn't show every extreme that they name: `clip_label`: clip numbers never fall along the frames; a clip's number is the index of its first frame; every clip holds at most 64 frames, and some clip holds exactly 64; the last frame forms a clip of its own.
All inputs are finite; a program needn't handle non-finite values.
Results may differ from the reference program's by a relative error of at most 0.0003.
Values may be sent and summed in bfloat16 or wider, within the bound.
A program may use at most 64 MiB of HBM per device.

```python
import math
import jax
import jax.numpy as jnp
from jax import lax

EMBED_WIDTH = 1024
SLAB_FRAMES = 2048
CLIP_MOST = 64
REACH = 1
FRAMES = 8192
N_BLK = 4


def clip_table(key):
    position = jnp.arange(FRAMES, dtype=jnp.int32)
    phase = jax.random.randint(jax.random.fold_in(key, 13), (), 1, CLIP_MOST).astype(jnp.int32)
    rolled = jax.random.randint(jax.random.fold_in(key, 11), (FRAMES,), 0, 24)
    periodic = (position + phase) % CLIP_MOST == 0
    extra = (rolled == 0) & (position >= 2 * CLIP_MOST)
    starts = periodic | extra | (position == 0) | (position == FRAMES - 1)
    first_index = jnp.where(starts, position, 0).astype(jnp.int32)
    return lax.cummax(first_index, axis=0).astype(jnp.int32)


def draw_clip_label(key, part):
    return clip_table(key)


def draw_frames(key, part):
    labels = clip_table(key)
    subkeys = jax.random.split(jax.random.fold_in(key, 23), 2)
    shared = jax.random.truncated_normal(subkeys[0], -4.0, 4.0, (FRAMES, EMBED_WIDTH), jnp.float32)
    noise_part = jax.random.truncated_normal(subkeys[1], -4.0, 4.0, (FRAMES, EMBED_WIDTH), jnp.float32)
    values = 0.8 * shared[labels] + 0.6 * noise_part
    return values.astype(jnp.bfloat16)


def setup_inputs(seed: int = 0, part: int = 0) -> dict:
    streams_of = jax.random.split(jax.random.key(seed), 3)
    own_keys = jax.random.split(jax.random.fold_in(streams_of[2], part), 3)
    return {
        "frames": draw_frames(jax.random.fold_in(jax.random.fold_in(streams_of[2], part), 71), part),
        "clip_label": draw_clip_label(jax.random.fold_in(jax.random.fold_in(streams_of[2], part), 71), part),
    }


softness_level = 0.5
masked_value = -1e+30

def reference(frames, clip_label):
    slabs_in_window = 2 * REACH + 1
    scale_factor = 1.0 / (math.sqrt(EMBED_WIDTH) * softness_level)
    doubled = jnp.concatenate([frames, frames], axis=0)
    doubled_label = jnp.concatenate([clip_label, clip_label], axis=0)

    def one_slab(slab_index):
        rows_of_slab = lax.dynamic_slice_in_dim(frames, slab_index * SLAB_FRAMES, SLAB_FRAMES, 0)
        row_label = lax.dynamic_slice_in_dim(clip_label, slab_index * SLAB_FRAMES, SLAB_FRAMES, 0)
        window_start = (slab_index - REACH) % N_BLK * SLAB_FRAMES
        window_keys = lax.dynamic_slice_in_dim(doubled, window_start, slabs_in_window * SLAB_FRAMES, 0)
        key_label = lax.dynamic_slice_in_dim(doubled_label, window_start, slabs_in_window * SLAB_FRAMES, 0)
        similarity = lax.dot_general(rows_of_slab, window_keys, (((1,), (1,)), ((), ())), preferred_element_type=jnp.float32) * scale_factor
        kept_pair = row_label[:, None] != key_label[None, :]
        row_maximum = lax.optimization_barrier(jnp.max(jnp.where(kept_pair, similarity, masked_value), axis=1))
        row_sum_value = lax.optimization_barrier(jnp.sum(jnp.where(kept_pair, jnp.exp(similarity - row_maximum[:, None]), 0.0), axis=1))
        return softness_level * (row_maximum + jnp.log(row_sum_value) - math.log(slabs_in_window * SLAB_FRAMES))
    scores = lax.map(one_slab, jnp.arange(N_BLK, dtype=jnp.int32))
    return scores.reshape(FRAMES)
```

```python
import functools
import math

import jax
import jax.numpy as jnp
from jax import lax
from jax.experimental import pallas as pl
from jax.experimental.pallas import tpu as pltpu
from jax.sharding import PartitionSpec as P

softness_level = 0.5
masked_value = -1e30
MESH = pl.DeviceIdType.MESH
LANES = 128
ROW_BLOCK = 256


def kernel(
    sizes,
    x_ref,
    label_hbm,
    out_ref,
    queries,
    partner_keys,
    next_keys,
    labels,
    label_ref,
    query_label,
    row_peak,
    row_total,
    col_peak,
    col_total,
    row_parts,
    col_out,
    col_parts,
    local_sem,
    label_sem,
    x_send,
    x_recv,
    z_send,
    z_recv,
    own_send,
    own_recv,
    fwd_send,
    fwd_recv,
    label_send,
    label_recv,
    row_send,
    row_recv,
    col_send,
    col_recv,
):
    cycle, feats, reach, rows, width, chunk = sizes
    piece = rows // feats
    n_key = piece // chunk
    n_all = rows // chunk
    factor = math.log2(math.e) / (math.sqrt(width * feats) * softness_level)
    blk = lax.axis_index("blk")
    feat = lax.axis_index("feat")
    sub = lax.axis_index("sub")
    other = 1 - sub

    def ahead(d):
        return lax.rem(blk + d, cycle)

    def behind(d):
        return lax.rem(blk + cycle - d, cycle)

    def peer(o):
        return lax.rem(feat + o, feats)

    def chunk_rows(owner, k):
        start = lax.rem(owner * piece + k * chunk, rows)
        return pl.ds(pl.multiple_of(start, chunk), chunk)

    def cols(q):
        return pl.ds(pl.multiple_of(q * width, width), width)

    def features(q, r):
        return queries.at[r, cols(q)]

    def send(src, dst, ssem, rsem, **where):
        return pltpu.make_async_remote_copy(
            src_ref=src, dst_ref=dst, send_sem=ssem, recv_sem=rsem,
            device_id=where, device_id_type=MESH,
        )

    key_rows = pl.ds(pl.multiple_of(feat * piece, piece), piece)

    def x_copy(o, k):
        to = peer(o)
        r = chunk_rows(to, k)
        return send(x_ref.at[r], features(feat, r), x_send.at[o, k], x_recv.at[feat, k], feat=to)

    def x_arrival(o, k):
        q = peer(o)
        r = chunk_rows(feat, k)
        return send(x_ref.at[r], features(q, r), x_send.at[o, k], x_recv.at[q, k], feat=q)

    def key_part(q, k, held):
        r = chunk_rows(feat, k)
        return features(q, r) if held else x_ref.at[r]

    def z_copy(d, q, k, held):
        return send(
            key_part(q, k, held), next_keys.at[d - 1, k, sub, :, cols(q)],
            z_send.at[d - 1, q, k], z_recv.at[d - 1, q, k], blk=ahead(d),
        )

    def own_copy(q, k, held):
        return send(
            key_part(q, k, held), partner_keys.at[pl.ds(k * chunk, chunk), cols(q)],
            own_send.at[q, k], own_recv.at[q, k], sub=other,
        )

    def fwd_copy(d, q, k, origin):
        part = next_keys.at[d - 1, k, origin, :, cols(q)]
        return send(
            part, part, fwd_send.at[d - 1, q, k], fwd_recv.at[d - 1, q, k], sub=other
        )

    def label_slot(d, origin):
        return 1 + 2 * (d - 1) + origin

    def label_copy(d, turn, slot):
        to = sub if turn == 0 else other
        return send(
            label_hbm, labels.at[slot], label_send.at[label_slot(d, turn)],
            label_recv.at[slot], blk=ahead(d), sub=to,
        )

    def partner_label():
        return send(label_hbm, labels.at[0], label_send.at[0], label_recv.at[0], sub=other)

    def row_copy(o, slot):
        return send(
            row_parts.at[slot], row_parts.at[slot], row_send.at[o], row_recv.at[slot],
            feat=peer(o),
        )

    def col_copy(d, f, t, slot_f, slot_s):
        return send(
            col_out.at[d - 1, t], col_parts.at[d - 1, slot_f, slot_s],
            col_send.at[d - 1, f, t], col_recv.at[d - 1, slot_f, slot_s],
            blk=behind(d), feat=f, sub=t,
        )

    local = pltpu.make_async_copy(x_ref, queries.at[:, cols(feat)], local_sem)
    local.start()
    local_label = pltpu.make_async_copy(label_hbm, label_ref, label_sem)
    local_label.start()

    barrier = pltpu.get_barrier_semaphore()
    pl.semaphore_signal(barrier, inc=1, device_id={"sub": other}, device_id_type=MESH)
    for o in range(1, feats):
        pl.semaphore_signal(barrier, inc=1, device_id={"feat": peer(o)}, device_id_type=MESH)
    for d in range(1, reach + 1):
        for t in range(2):
            pl.semaphore_signal(
                barrier, inc=1, device_id={"blk": behind(d), "sub": t}, device_id_type=MESH
            )
    pl.semaphore_wait(barrier, feats + 2 * reach)

    sends = []

    def go(copy):
        copy.start()
        sends.append(copy)

    for k in range(n_all):
        for o in range(1, feats):
            go(x_copy(o, k))
        if k < n_key:
            for d in range(1, reach + 1):
                go(z_copy(d, feat, k, False))
            go(own_copy(feat, k, False))
    go(partner_label())
    for d in range(1, reach + 1):
        for turn in range(2):
            go(label_copy(d, turn, label_slot(d, sub)))

    local_label.wait()
    row_peak[...] = jnp.full_like(row_peak, masked_value)
    row_total[...] = jnp.zeros_like(row_total)
    col_peak[...] = jnp.full_like(col_peak, masked_value)
    col_total[...] = jnp.zeros_like(col_total)
    for i in range(rows // LANES):
        line = label_ref[:, i * LANES : (i + 1) * LANES].astype(jnp.float32)
        query_label[i * LANES : (i + 1) * LANES, :] = jnp.broadcast_to(line, (LANES, LANES)).T

    def tile(start, count, keys, lines, column):
        groups = len(lines)
        block = min(ROW_BLOCK, count)
        parts = block // 8
        lane = [slice(b * LANES, (b + 1) * LANES) for b in range(groups)]

        def one(i, carry):
            there = pl.ds(pl.multiple_of(start + i * block, block), block)
            score = lax.dot_general(
                queries[there, :], keys(), (((1,), (1,)), ((), ())),
                preferred_element_type=jnp.float32,
            )
            mine = query_label[there, :]
            values = [
                jnp.where(mine != lines[b], score[:, lane[b]] * factor, masked_value)
                for b in range(groups)
            ]
            old = row_peak[there, :]
            new = functools.reduce(jnp.maximum, values, old)
            row_peak[there, :] = new
            row_total[there, :] = functools.reduce(
                jnp.add,
                [jnp.exp2(v - new) for v in values],
                row_total[there, :] * jnp.exp2(old - new),
            )
            if column is not None:
                d, j = column
                for b in range(groups):
                    v = values[b].reshape(parts, 8, LANES)
                    old_c = col_peak[d - 1, j, :, lane[b]]
                    new_c = jnp.maximum(old_c, jnp.max(v, axis=0))
                    col_peak[d - 1, j, :, lane[b]] = new_c
                    col_total[d - 1, j, :, lane[b]] = col_total[
                        d - 1, j, :, lane[b]
                    ] * jnp.exp2(old_c - new_c) + jnp.sum(jnp.exp2(v - new_c[None]), axis=0)
            return carry

        lax.fori_loop(0, count // block, one, 0, unroll=True)

    for k in range(n_key):
        for o in range(1, feats):
            q = peer(o)
            x_arrival(o, k).wait_recv()
            for d in range(1, reach + 1):
                go(z_copy(d, q, k, True))
            go(own_copy(q, k, True))
    for k in range(n_key):
        for d in range(1, reach + 1):
            z_copy(d, feat, k, False).wait_recv()
            go(fwd_copy(d, feat, k, sub))

    local.wait()
    partner_label().wait_recv()
    for d in range(1, reach + 1):
        label_copy(d, 0, label_slot(d, sub)).wait_recv()
        label_copy(d, 1, label_slot(d, other)).wait_recv()

    def key_lines(line):
        return [line[:, b * LANES : (b + 1) * LANES] for b in range(line.shape[1] // LANES)]

    own_lines = key_lines(label_ref[:, key_rows].astype(jnp.float32))
    beside_lines = key_lines(labels[0, :, key_rows].astype(jnp.float32))
    first_row = pl.multiple_of(feat * piece, piece)

    def own_tile(start, count):
        tile(start, count, lambda: queries[key_rows, :], own_lines, None)

    def beside_tile(start, count):
        tile(start, count, lambda: partner_keys[...], beside_lines, None)

    def next_tile(start, count, d, j):
        r = pl.ds(pl.multiple_of(feat * piece + j * chunk, chunk), chunk)
        lines = []
        for t in range(2):
            lines += key_lines(labels[label_slot(d, t), :, r].astype(jnp.float32))
        keys = lambda: next_keys[d - 1, j].reshape(2 * chunk, width * feats)
        tile(start, count, keys, lines, (d, j))

    def rotated(k):
        return pl.multiple_of(lax.rem(feat * piece + k * chunk, rows), chunk)

    own_tile(first_row, piece)
    for k in range(n_key):
        for q in range(feats):
            own_copy(q, k, False).wait_recv()
    beside_tile(first_row, piece)

    def relay(j):
        for d in range(1, reach + 1):
            for o in range(1, feats):
                z_copy(d, peer(o), j, False).wait_recv()
                go(fwd_copy(d, peer(o), j, sub))

    def key_chunk(j, upto):
        for d in range(1, reach + 1):
            for q in range(feats):
                fwd_copy(d, q, j, other).wait_recv()
            tall = max(h for h in range(1, n_key + 1) if upto % h == 0 and n_key % h == 0)

            def step(i, carry):
                next_tile(rotated(i * tall), tall * chunk, d, j)
                return carry

            lax.fori_loop(0, upto // tall, step, 0, unroll=True)

    relayed, scored, owned = 0, 0, n_key
    for k in range(n_key, n_all):
        if scored < relayed:
            key_chunk(scored, k)
            scored += 1
        for o in range(1, feats):
            x_arrival(o, k).wait_recv()
        if relayed < n_key:
            relay(relayed)
            relayed += 1
        start = rotated(k)
        for d in range(1, reach + 1):
            for j in range(scored):
                next_tile(start, chunk, d, j)
        if n_key % 2 == 0 and k + 1 - owned == 2 and k + 1 < n_all:
            own_tile(rotated(owned), 2 * chunk)
            beside_tile(rotated(owned), 2 * chunk)
            owned += 2
    while relayed < n_key:
        relay(relayed)
        relayed += 1
    left = 2 if n_key % 2 == 0 else 1
    for k in range(owned, n_all, left):
        own_tile(rotated(k), left * chunk)
        beside_tile(rotated(k), left * chunk)
    while scored < n_key:
        key_chunk(scored, n_all)
        scored += 1

    for d in range(1, reach + 1):
        for t in range(2):
            for j in range(n_key):
                part = slice(t * chunk, (t + 1) * chunk)
                peaks = col_peak[d - 1, j, :, part]
                top = jnp.max(peaks, axis=0, keepdims=True)
                total = jnp.sum(
                    col_total[d - 1, j, :, part] * jnp.exp2(peaks - top), axis=0, keepdims=True
                )
                col_out[d - 1, t, :, j * chunk : (j + 1) * chunk] = (
                    top * math.log(2.0) + jnp.log(total)
                )
            for f in range(feats):
                go(col_copy(d, f, t, feat, sub))
    for i in range(rows // LANES):
        here = slice(i * LANES, (i + 1) * LANES)
        peaks = row_peak[here, :].T
        top = jnp.max(peaks, axis=0, keepdims=True)
        total = jnp.sum(row_total[here, :].T * jnp.exp2(peaks - top), axis=0, keepdims=True)
        row_parts[feat, :, here] = top * math.log(2.0) + jnp.log(total)
    for o in range(1, feats):
        go(row_copy(o, feat))

    for o in range(1, feats):
        row_copy(o, peer(o)).wait_recv()
    for d in range(1, reach + 1):
        for f in range(feats):
            for t in range(2):
                col_copy(d, f, t, f, t).wait_recv()

    shift = math.log((2 * reach + 1) * rows * 2)
    for f in range(feats):
        here = slice(f * piece, (f + 1) * piece)
        parts = [row_parts[q, :, here] for q in range(feats)]
        parts += [col_parts[d, f, t] for d in range(reach) for t in range(2)]
        top = functools.reduce(jnp.maximum, parts)
        total = functools.reduce(jnp.add, [jnp.exp(v - top) for v in parts])
        out_ref[:, here] = softness_level * (top + jnp.log(total) - shift)

    for copy in sends:
        copy.wait_send()


def solution(mesh):
    cycle, feats = mesh.shape["blk"], mesh.shape["feat"]
    reach = min(4, (cycle - 1) // 2)

    def body(frames, clip_label):
        rows, width = frames.shape
        piece = rows // feats
        chunk = min(128, piece)
        n_key, n_all = piece // chunk, rows // chunk
        dma = pltpu.SemaphoreType.DMA
        sizes = (cycle, feats, reach, rows, width, chunk)
        out = pl.pallas_call(
            functools.partial(kernel, sizes),
            out_shape=jax.ShapeDtypeStruct((1, rows), jnp.float32),
            in_specs=[
                pl.BlockSpec(memory_space=pltpu.HBM),
                pl.BlockSpec(memory_space=pltpu.HBM),
            ],
            out_specs=pl.BlockSpec(memory_space=pltpu.VMEM),
            scratch_shapes=[
                pltpu.VMEM((rows, feats * width), frames.dtype),
                pltpu.VMEM((piece, feats * width), frames.dtype),
                pltpu.VMEM((reach, n_key, 2, chunk, feats * width), frames.dtype),
                pltpu.VMEM((1 + 2 * reach, 1, rows), jnp.int32),
                pltpu.VMEM((1, rows), jnp.int32),
                pltpu.VMEM((rows, LANES), jnp.float32),
                pltpu.VMEM((rows, LANES), jnp.float32),
                pltpu.VMEM((rows, LANES), jnp.float32),
                pltpu.VMEM((reach, n_key, 8, 2 * chunk), jnp.float32),
                pltpu.VMEM((reach, n_key, 8, 2 * chunk), jnp.float32),
                pltpu.VMEM((feats, 1, rows), jnp.float32),
                pltpu.VMEM((reach, 2, 1, piece), jnp.float32),
                pltpu.VMEM((reach, feats, 2, 1, piece), jnp.float32),
                dma,
                dma,
                dma((feats, n_all)),
                dma((feats, n_all)),
                dma((reach, feats, n_key)),
                dma((reach, feats, n_key)),
                dma((feats, n_key)),
                dma((feats, n_key)),
                dma((reach, feats, n_key)),
                dma((reach, feats, n_key)),
                dma((1 + 2 * reach,)),
                dma((1 + 2 * reach,)),
                dma((feats,)),
                dma((feats,)),
                dma((reach, feats, 2)),
                dma((reach, feats, 2)),
            ],
            compiler_params=pltpu.CompilerParams(
                collective_id=0, has_side_effects=True, vmem_limit_bytes=63 * 1024 * 1024
            ),
            name="chamfer",
        )(frames, clip_label.reshape(1, rows))
        return out.reshape(rows)

    in_specs = (P(("groups", "blk", "sub"), "feat"), P(("groups", "blk", "sub")))
    out_specs = P(("groups", "blk", "sub"))
    return jax.shard_map(body, mesh=mesh, in_specs=in_specs, out_specs=out_specs, check_vma=False)
```

```python
import functools
import math

import jax
import jax.numpy as jnp
from jax import lax
from jax.experimental import pallas as pl
from jax.experimental.pallas import tpu as pltpu
from jax.sharding import PartitionSpec as P

softness_level = 0.5
masked_value = -1e30
MESH = pl.DeviceIdType.MESH
LANES = 128
KEY_BLOCK = 256


def kernel(
    sizes,
    x_ref,
    label_hbm,
    out_ref,
    queries,
    next_keys,
    labels,
    query_line,
    own_label,
    next_label,
    row_peak,
    row_total,
    col_peak,
    col_total,
    row_out,
    row_parts,
    col_out,
    col_parts,
    local_sem,
    x_send,
    x_recv,
    z_send,
    z_recv,
    sub_send,
    sub_recv,
    label_send,
    label_recv,
    row_send,
    row_recv,
    col_send,
    col_recv,
):
    cycle, feats, reach, rows, width, chunk = sizes
    piece = rows // feats
    n_key = piece // chunk
    n_all = rows // chunk
    group = 2 if n_key % 2 == 0 else 1
    factor = math.log2(math.e) / (math.sqrt(width * feats) * softness_level)
    blk = lax.axis_index("blk")
    feat = lax.axis_index("feat")
    sub = lax.axis_index("sub")
    other = 1 - sub

    def ahead(d):
        return lax.rem(blk + d, cycle)

    def behind(d):
        return lax.rem(blk + cycle - d, cycle)

    def peer(o):
        return lax.rem(feat + o, feats)

    def chunk_rows(owner, k, count=1):
        start = lax.rem(owner * piece + k * chunk, rows)
        return pl.ds(pl.multiple_of(start, chunk * count), chunk * count)

    def cols(q):
        return pl.ds(pl.multiple_of(q * width, width), width)

    def send(src, dst, ssem, rsem, **where):
        return pltpu.make_async_remote_copy(
            src_ref=src, dst_ref=dst, send_sem=ssem, recv_sem=rsem,
            device_id=where, device_id_type=MESH,
        )

    def x_copy(o, k):
        to = peer(o)
        r = chunk_rows(to, k)
        return send(
            x_ref.at[r], queries.at[0, r, cols(feat)], x_send.at[o, k], x_recv.at[feat, k],
            feat=to,
        )

    def x_arrival(o, k):
        q = peer(o)
        r = chunk_rows(feat, k)
        return send(
            x_ref.at[r], queries.at[0, r, cols(q)], x_send.at[o, k], x_recv.at[q, k], feat=q
        )

    def part(q, k, held):
        r = chunk_rows(feat, k)
        return queries.at[0, r, cols(q)] if held else x_ref.at[r]

    def z_copy(d, q, k, held):
        return send(
            part(q, k, held), next_keys.at[d - 1, k, :, cols(q)],
            z_send.at[d - 1, q, k], z_recv.at[d - 1, q, k], blk=ahead(d),
        )

    def sub_copy(q, k, held):
        return send(
            part(q, k, held), queries.at[1, chunk_rows(feat, k), cols(q)],
            sub_send.at[q, k], sub_recv.at[q, k], sub=other,
        )

    def label_copy(slot):
        where = {"sub": other} if slot == 1 else {"blk": ahead(slot - 1)}
        return send(label_hbm, labels.at[slot], label_send.at[slot], label_recv.at[slot], **where)

    def row_copy(o, half, slot_f, slot_s):
        src = row_out if half else row_parts.at[slot_f, slot_s]
        return send(
            src, row_parts.at[slot_f, slot_s], row_send.at[o, half], row_recv.at[slot_f, slot_s],
            feat=peer(o), sub=other if half else sub,
        )

    def col_copy(d, f, slot_f):
        return send(
            col_out.at[d - 1], col_parts.at[d - 1, slot_f], col_send.at[d - 1, f],
            col_recv.at[d - 1, slot_f], blk=behind(d), feat=f,
        )

    local = pltpu.make_async_copy(x_ref, queries.at[0, :, cols(feat)], local_sem.at[0])
    local.start()
    local_label = pltpu.make_async_copy(label_hbm, labels.at[0], local_sem.at[1])
    local_label.start()

    barrier = pltpu.get_barrier_semaphore()
    pl.semaphore_signal(barrier, inc=1, device_id={"sub": other}, device_id_type=MESH)
    for o in range(1, feats):
        pl.semaphore_signal(barrier, inc=1, device_id={"feat": peer(o)}, device_id_type=MESH)
    for d in range(1, reach + 1):
        pl.semaphore_signal(barrier, inc=1, device_id={"blk": behind(d)}, device_id_type=MESH)
    pl.semaphore_wait(barrier, feats + reach)

    sends = []

    def go(copy):
        copy.start()
        sends.append(copy)

    for k in range(n_all):
        for o in range(1, feats):
            go(x_copy(o, k))
        if k < n_key:
            for d in range(1, reach + 1):
                go(z_copy(d, feat, k, False))
    for slot in range(1, 2 + reach):
        go(label_copy(slot))
    for k in range(n_all):
        go(sub_copy(feat, k, False))

    row_peak[...] = jnp.full_like(row_peak, masked_value)
    row_total[...] = jnp.zeros_like(row_total)
    col_peak[...] = jnp.full_like(col_peak, masked_value)
    col_total[...] = jnp.zeros_like(col_total)

    def down(slot, k):
        line = labels[slot, :, chunk_rows(feat, k)].astype(jnp.float32)
        return jnp.broadcast_to(line, (LANES, chunk)).T

    def across(slot, s):
        for k in range(n_all):
            line = labels[slot, :, chunk_rows(feat, k)].astype(jnp.float32)
            query_line[s, k] = jnp.broadcast_to(line, (8, chunk))

    def tile(s, u, keys, key_label, column):
        count = keys.shape[0]
        block = min(KEY_BLOCK, count)
        q = queries[s, chunk_rows(feat, u * group, group), :]
        lane = [slice(b * chunk, (b + 1) * chunk) for b in range(group)]
        for m in range(0, count, block):
            here = slice(m, m + block)
            score = lax.dot_general(
                keys[here, :], q, (((1,), (1,)), ((), ())), preferred_element_type=jnp.float32
            )
            mine = key_label[here, :]
            values = []
            for b in range(group):
                k = u * group + b
                line = query_line[s, k]
                apart = mine.reshape(block // 8, 8, chunk) != line[None]
                v = jnp.where(
                    apart, (score[:, lane[b]] * factor).reshape(block // 8, 8, chunk), masked_value
                )
                values.append(v)
                old = row_peak[s, k]
                new = jnp.maximum(old, jnp.max(v, axis=0))
                row_peak[s, k] = new
                row_total[s, k] = row_total[s, k] * jnp.exp2(old - new) + jnp.sum(
                    jnp.exp2(v - new[None]), axis=0
                )
            if column is not None:
                peak, total = column
                values = [v.reshape(block, chunk) for v in values]
                old = peak[here, :]
                new = functools.reduce(jnp.maximum, values, old)
                peak[here, :] = new
                total[here, :] = functools.reduce(
                    jnp.add,
                    [jnp.exp2(v - new) for v in values],
                    total[here, :] * jnp.exp2(old - new),
                )

    def own_tile(s, u):
        tile(s, u, queries.at[0, chunk_rows(feat, 0, n_key)], own_label, None)

    def next_tile(s, u, d, j):
        here = pl.ds(j * chunk, chunk)
        tile(
            s, u, next_keys.at[d - 1, j], next_label.at[d - 1, here],
            (col_peak.at[d - 1, here], col_total.at[d - 1, here]),
        )

    done, taken = [], []

    def take_x(k):
        for o in range(1, feats):
            q = peer(o)
            x_arrival(o, k).wait_recv()
            if k < n_key:
                for d in range(1, reach + 1):
                    go(z_copy(d, q, k, True))
            go(sub_copy(q, k, True))

    def take_sub(k):
        for o in range(feats):
            sub_copy(peer(o), k, False).wait_recv()

    def take_queries(s, units):
        for u in units:
            own_tile(s, u)
            for d, j in taken:
                next_tile(s, u, d, j)
            done.append((s, u))

    def take_keys(j):
        for d in range(1, reach + 1):
            for q in range(feats):
                z_copy(d, q, j, False).wait_recv()
            for s, u in done:
                next_tile(s, u, d, j)
            taken.append((d, j))

    def finish_columns(j):
        for d in range(1, reach + 1):
            here = pl.ds(j * chunk, chunk)
            peaks = col_peak[d - 1, here, :].T
            top = jnp.max(peaks, axis=0, keepdims=True)
            total = jnp.sum(
                col_total[d - 1, here, :].T * jnp.exp2(peaks - top), axis=0, keepdims=True
            )
            col_out[d - 1, :, here] = top * math.log(2.0) + jnp.log(total)

    def finish_rows(s):
        for k in range(n_all):
            peaks = row_peak[s, k]
            top = jnp.max(peaks, axis=0, keepdims=True)
            total = jnp.sum(row_total[s, k] * jnp.exp2(peaks - top), axis=0, keepdims=True)
            value = top * math.log(2.0) + jnp.log(total)
            if s:
                row_out[:, chunk_rows(feat, k)] = value
            else:
                row_parts[feat, sub, :, chunk_rows(feat, k)] = value

    local_label.wait()
    across(0, 0)
    for k in range(n_key):
        own_label[k * chunk : (k + 1) * chunk, :] = down(0, k)
    label_copy(1).wait_recv()
    across(1, 1)
    for d in range(1, reach + 1):
        label_copy(1 + d).wait_recv()
        for k in range(n_key):
            next_label[d - 1, k * chunk : (k + 1) * chunk, :] = down(1 + d, k)

    for k in range(n_key):
        take_x(k)
    local.wait()
    first = range(n_key // group)
    take_queries(0, first)
    for k in range(n_key):
        take_sub(k)
    take_queries(1, first)

    steps = (n_all - n_key) // group
    ready = 0

    def catch_up(upto):
        nonlocal ready
        while ready < upto:
            take_keys(ready)
            ready += 1

    for i in range(steps):
        u = n_key // group + i
        for b in range(group):
            if b == group - 1 and i == steps - 1:
                catch_up(n_key - 1)
            take_x(u * group + b)
        take_queries(0, [u])
        for b in range(group):
            take_sub(u * group + b)
        take_queries(1, [u])
        catch_up(n_key * (i + 1) // steps if i < steps - 1 else n_key - 1)
    for j in range(n_key - 1):
        finish_columns(j)
    catch_up(n_key)

    finish_rows(1)
    for o in range(feats):
        go(row_copy(o, 1, feat, sub))
    finish_rows(0)
    for o in range(1, feats):
        go(row_copy(o, 0, feat, sub))
    finish_columns(n_key - 1)
    for d in range(1, reach + 1):
        for f in range(feats):
            go(col_copy(d, f, feat))

    for o in range(feats):
        for s in range(2):
            if o or s:
                row_copy(o, s, peer(o), other if s else sub).wait_recv()
    for d in range(1, reach + 1):
        for f in range(feats):
            col_copy(d, f, f).wait_recv()

    shift = math.log((2 * reach + 1) * rows * 2)
    for f in range(feats):
        here = slice(f * piece, (f + 1) * piece)
        parts = [row_parts[q, s, :, here] for q in range(feats) for s in range(2)]
        parts += [col_parts[d, f] for d in range(reach)]
        top = functools.reduce(jnp.maximum, parts)
        total = functools.reduce(jnp.add, [jnp.exp(v - top) for v in parts])
        out_ref[:, here] = softness_level * (top + jnp.log(total) - shift)

    for copy in sends:
        copy.wait_send()


def solution(mesh):
    cycle, feats = mesh.shape["blk"], mesh.shape["feat"]
    reach = min(4, (cycle - 1) // 2)

    def body(frames, clip_label):
        rows, width = frames.shape
        piece = rows // feats
        chunk = min(LANES, piece)
        n_key, n_all = piece // chunk, rows // chunk
        dma = pltpu.SemaphoreType.DMA
        f32 = jnp.float32
        sizes = (cycle, feats, reach, rows, width, chunk)
        out = pl.pallas_call(
            functools.partial(kernel, sizes),
            out_shape=jax.ShapeDtypeStruct((1, rows), f32),
            in_specs=[
                pl.BlockSpec(memory_space=pltpu.HBM),
                pl.BlockSpec(memory_space=pltpu.HBM),
            ],
            out_specs=pl.BlockSpec(memory_space=pltpu.VMEM),
            scratch_shapes=[
                pltpu.VMEM((2, rows, feats * width), frames.dtype),
                pltpu.VMEM((reach, n_key, chunk, feats * width), frames.dtype),
                pltpu.VMEM((2 + reach, 1, rows), jnp.int32),
                pltpu.VMEM((2, n_all, 8, chunk), f32),
                pltpu.VMEM((piece, LANES), f32),
                pltpu.VMEM((reach, piece, LANES), f32),
                pltpu.VMEM((2, n_all, 8, chunk), f32),
                pltpu.VMEM((2, n_all, 8, chunk), f32),
                pltpu.VMEM((reach, piece, LANES), f32),
                pltpu.VMEM((reach, piece, LANES), f32),
                pltpu.VMEM((1, rows), f32),
                pltpu.VMEM((feats, 2, 1, rows), f32),
                pltpu.VMEM((reach, 1, piece), f32),
                pltpu.VMEM((reach, feats, 1, piece), f32),
                dma((2,)),
                dma((feats, n_all)),
                dma((feats, n_all)),
                dma((reach, feats, n_key)),
                dma((reach, feats, n_key)),
                dma((feats, n_all)),
                dma((feats, n_all)),
                dma((2 + reach,)),
                dma((2 + reach,)),
                dma((feats, 2)),
                dma((feats, 2)),
                dma((reach, feats)),
                dma((reach, feats)),
            ],
            compiler_params=pltpu.CompilerParams(
                collective_id=0, has_side_effects=True, vmem_limit_bytes=63 * 1024 * 1024
            ),
            name="chamfer",
        )(frames, clip_label.reshape(1, rows))
        return out.reshape(rows)

    in_specs = (P(("groups", "blk", "sub"), "feat"), P(("groups", "blk", "sub")))
    out_specs = P(("groups", "blk", "sub"))
    return jax.shard_map(body, mesh=mesh, in_specs=in_specs, out_specs=out_specs, check_vma=False)
```

```python
import functools
import math

import jax
import jax.numpy as jnp
from jax import lax
from jax.experimental import pallas as pl
from jax.experimental.pallas import tpu as pltpu
from jax.sharding import PartitionSpec as P

softness_level = 0.5
masked_value = -1e30
MESH = pl.DeviceIdType.MESH
LANES = 128
KEY_BLOCK = 256


def kernel(
    sizes,
    x_ref,
    label_hbm,
    out_ref,
    queries,
    next_keys,
    labels,
    query_line,
    own_label,
    next_label,
    row_peak,
    row_total,
    col_peak,
    col_total,
    row_out,
    row_parts,
    col_out,
    col_parts,
    local_sem,
    x_send,
    x_recv,
    z_send,
    z_recv,
    sub_send,
    sub_recv,
    label_send,
    label_recv,
    row_send,
    row_recv,
    col_send,
    col_recv,
):
    cycle, feats, reach, rows, width, chunk = sizes
    piece = rows // feats
    n_key = piece // chunk
    n_all = rows // chunk
    factor = math.log2(math.e) / (math.sqrt(width * feats) * softness_level)
    blk = lax.axis_index("blk")
    feat = lax.axis_index("feat")
    sub = lax.axis_index("sub")
    other = 1 - sub

    def ahead(d):
        return lax.rem(blk + d, cycle)

    def behind(d):
        return lax.rem(blk + cycle - d, cycle)

    def peer(o):
        return lax.rem(feat + o, feats)

    def chunk_rows(owner, k, count=1):
        start = lax.rem(owner * piece + k * chunk, rows)
        return pl.ds(pl.multiple_of(start, chunk * count), chunk * count)

    def cols(q):
        return pl.ds(pl.multiple_of(q * width, width), width)

    def send(src, dst, ssem, rsem, **where):
        return pltpu.make_async_remote_copy(
            src_ref=src, dst_ref=dst, send_sem=ssem, recv_sem=rsem,
            device_id=where, device_id_type=MESH,
        )

    def x_copy(o, k):
        to = peer(o)
        r = chunk_rows(to, k)
        return send(
            x_ref.at[r], queries.at[0, r, cols(feat)], x_send.at[o, k], x_recv.at[feat, k],
            feat=to,
        )

    def x_arrival(o, k):
        q = peer(o)
        r = chunk_rows(feat, k)
        return send(
            x_ref.at[r], queries.at[0, r, cols(q)], x_send.at[o, k], x_recv.at[q, k], feat=q
        )

    def part(q, k, held):
        r = chunk_rows(feat, k)
        return queries.at[0, r, cols(q)] if held else x_ref.at[r]

    def z_copy(d, q, k, held):
        return send(
            part(q, k, held), next_keys.at[d - 1, pl.ds(k * chunk, chunk), cols(q)],
            z_send.at[d - 1, q, k], z_recv.at[d - 1, q, k], blk=ahead(d),
        )

    def sub_copy(q, k, held):
        return send(
            part(q, k, held), queries.at[1, chunk_rows(feat, k), cols(q)],
            sub_send.at[q, k], sub_recv.at[q, k], sub=other,
        )

    def label_copy(slot):
        where = {"sub": other} if slot == 1 else {"blk": ahead(slot - 1)}
        return send(label_hbm, labels.at[slot], label_send.at[slot], label_recv.at[slot], **where)

    def row_copy(o, half, slot_f, slot_s):
        src = row_out if half else row_parts.at[slot_f, slot_s]
        return send(
            src, row_parts.at[slot_f, slot_s], row_send.at[o, half], row_recv.at[slot_f, slot_s],
            feat=peer(o), sub=other if half else sub,
        )

    def col_copy(d, f, slot_f):
        return send(
            col_out.at[d - 1], col_parts.at[d - 1, slot_f], col_send.at[d - 1, f],
            col_recv.at[d - 1, slot_f], blk=behind(d), feat=f,
        )

    local = pltpu.make_async_copy(x_ref, queries.at[0, :, cols(feat)], local_sem.at[0])
    local.start()
    local_label = pltpu.make_async_copy(label_hbm, labels.at[0], local_sem.at[1])
    local_label.start()

    barrier = pltpu.get_barrier_semaphore()
    pl.semaphore_signal(barrier, inc=1, device_id={"sub": other}, device_id_type=MESH)
    for o in range(1, feats):
        pl.semaphore_signal(barrier, inc=1, device_id={"feat": peer(o)}, device_id_type=MESH)
    for d in range(1, reach + 1):
        pl.semaphore_signal(barrier, inc=1, device_id={"blk": behind(d)}, device_id_type=MESH)
    pl.semaphore_wait(barrier, feats + reach)

    sends = []

    def go(copy):
        copy.start()
        sends.append(copy)

    for slot in range(1, 2 + reach):
        go(label_copy(slot))
    for k in range(n_all):
        for o in range(1, feats):
            go(x_copy(o, k))
        if k < n_key:
            for d in range(1, reach + 1):
                go(z_copy(d, feat, k, False))
    for k in range(n_all):
        go(sub_copy(feat, k, False))

    row_peak[...] = jnp.full_like(row_peak, masked_value)
    row_total[...] = jnp.zeros_like(row_total)
    col_peak[...] = jnp.full_like(col_peak, masked_value)
    col_total[...] = jnp.zeros_like(col_total)

    def down(slot, k):
        line = labels[slot, :, chunk_rows(feat, k)].astype(jnp.float32)
        return jnp.broadcast_to(line, (LANES, chunk)).T

    def across(slot, s):
        for k in range(n_all):
            line = labels[slot, :, chunk_rows(feat, k)].astype(jnp.float32)
            query_line[s, k] = jnp.broadcast_to(line, (8, chunk))

    def tile(k, keys, key_label, column):
        count = keys.shape[0]
        q = queries[:, chunk_rows(feat, k), :].reshape(2 * chunk, width * feats)
        lane = [slice(s * chunk, (s + 1) * chunk) for s in range(2)]
        for m in range(0, count, KEY_BLOCK):
            block = min(KEY_BLOCK, count - m)
            here = slice(m, m + block)
            score = lax.dot_general(
                q, keys[here, :], (((1,), (1,)), ((), ())), preferred_element_type=jnp.float32
            ).T
            mine = key_label[here, :]
            values = []
            for s in range(2):
                apart = mine.reshape(block // 8, 8, chunk) != query_line[s, k][None]
                v = jnp.where(
                    apart, (score[:, lane[s]] * factor).reshape(block // 8, 8, chunk), masked_value
                )
                values.append(v)
                old = row_peak[s, k]
                new = jnp.maximum(old, jnp.max(v, axis=0))
                row_peak[s, k] = new
                row_total[s, k] = row_total[s, k] * jnp.exp2(old - new) + jnp.sum(
                    jnp.exp2(v - new[None]), axis=0
                )
            if column is not None:
                peak, total = column
                values = [v.reshape(block, chunk) for v in values]
                old = peak[here, :]
                new = functools.reduce(jnp.maximum, values, old)
                peak[here, :] = new
                total[here, :] = functools.reduce(
                    jnp.add,
                    [jnp.exp2(v - new) for v in values],
                    total[here, :] * jnp.exp2(old - new),
                )

    def own_tile(k):
        tile(k, queries.at[0, chunk_rows(feat, 0, n_key)], own_label, None)

    def next_tile(k, j, count):
        here = pl.ds(j * chunk, count * chunk)
        for d in range(1, reach + 1):
            tile(
                k, next_keys.at[d - 1, here], next_label.at[d - 1, here],
                (col_peak.at[d - 1, here], col_total.at[d - 1, here]),
            )

    def take_x(k):
        for o in range(1, feats):
            q = peer(o)
            x_arrival(o, k).wait_recv()
            if k < n_key:
                for d in range(1, reach + 1):
                    go(z_copy(d, q, k, True))
            go(sub_copy(q, k, True))

    def take_queries(k, ready):
        for o in range(feats):
            sub_copy(peer(o), k, False).wait_recv()
        own_tile(k)
        if ready:
            next_tile(k, 0, ready)

    def take_keys(j, upto):
        for d in range(1, reach + 1):
            for q in range(feats):
                z_copy(d, q, j, False).wait_recv()
        for k in range(upto):
            next_tile(k, j, 1)

    def finish_columns(j):
        for d in range(1, reach + 1):
            here = pl.ds(j * chunk, chunk)
            peaks = col_peak[d - 1, here, :].T
            top = jnp.max(peaks, axis=0, keepdims=True)
            total = jnp.sum(
                col_total[d - 1, here, :].T * jnp.exp2(peaks - top), axis=0, keepdims=True
            )
            col_out[d - 1, :, here] = top * math.log(2.0) + jnp.log(total)

    def finish_rows(s):
        for k in range(n_all):
            peaks = row_peak[s, k]
            top = jnp.max(peaks, axis=0, keepdims=True)
            total = jnp.sum(row_total[s, k] * jnp.exp2(peaks - top), axis=0, keepdims=True)
            value = top * math.log(2.0) + jnp.log(total)
            if s:
                row_out[:, chunk_rows(feat, k)] = value
            else:
                row_parts[feat, sub, :, chunk_rows(feat, k)] = value

    local_label.wait()
    across(0, 0)
    for k in range(n_key):
        own_label[k * chunk : (k + 1) * chunk, :] = down(0, k)

    for k in range(n_key):
        take_x(k)
        if k == 0:
            label_copy(1).wait_recv()
            across(1, 1)
            for d in range(1, reach + 1):
                label_copy(1 + d).wait_recv()
                for k in range(n_key):
                    next_label[d - 1, k * chunk : (k + 1) * chunk, :] = down(1 + d, k)
    local.wait()
    for k in range(n_key):
        take_queries(k, 0)

    ready, last_key, last = 0, n_key - 1, n_all - 1
    for k in range(n_key, last):
        take_x(k)
        upto = last_key * (k + 1 - n_key) // (last - n_key)
        while ready < upto:
            take_keys(ready, k)
            ready += 1
        take_queries(k, ready)
    while ready < last_key:
        take_keys(ready, last)
        ready += 1

    take_x(last)
    take_keys(last_key, last)
    take_queries(last, n_key)

    finish_rows(1)
    for o in range(feats):
        go(row_copy(o, 1, feat, sub))
    finish_rows(0)
    for o in range(1, feats):
        go(row_copy(o, 0, feat, sub))
    for j in range(n_key):
        finish_columns(j)
    for d in range(1, reach + 1):
        for f in range(feats):
            go(col_copy(d, f, feat))

    for o in range(feats):
        for s in range(2):
            if o or s:
                row_copy(o, s, peer(o), other if s else sub).wait_recv()
    for d in range(1, reach + 1):
        for f in range(feats):
            col_copy(d, f, f).wait_recv()

    shift = math.log((2 * reach + 1) * rows * 2)
    for f in range(feats):
        here = slice(f * piece, (f + 1) * piece)
        parts = [row_parts[q, s, :, here] for q in range(feats) for s in range(2)]
        parts += [col_parts[d, f] for d in range(reach)]
        top = functools.reduce(jnp.maximum, parts)
        total = functools.reduce(jnp.add, [jnp.exp(v - top) for v in parts])
        out_ref[:, here] = softness_level * (top + jnp.log(total) - shift)

    for copy in sends:
        copy.wait_send()


def solution(mesh):
    cycle, feats = mesh.shape["blk"], mesh.shape["feat"]
    reach = min(4, (cycle - 1) // 2)

    def body(frames, clip_label):
        rows, width = frames.shape
        piece = rows // feats
        chunk = min(LANES, piece)
        n_key, n_all = piece // chunk, rows // chunk
        dma = pltpu.SemaphoreType.DMA
        f32 = jnp.float32
        sizes = (cycle, feats, reach, rows, width, chunk)
        out = pl.pallas_call(
            functools.partial(kernel, sizes),
            out_shape=jax.ShapeDtypeStruct((1, rows), f32),
            in_specs=[
                pl.BlockSpec(memory_space=pltpu.HBM),
                pl.BlockSpec(memory_space=pltpu.HBM),
            ],
            out_specs=pl.BlockSpec(memory_space=pltpu.VMEM),
            scratch_shapes=[
                pltpu.VMEM((2, rows, feats * width), frames.dtype),
                pltpu.VMEM((reach, piece, feats * width), frames.dtype),
                pltpu.VMEM((2 + reach, 1, rows), jnp.int32),
                pltpu.VMEM((2, n_all, 8, chunk), f32),
                pltpu.VMEM((piece, LANES), f32),
                pltpu.VMEM((reach, piece, LANES), f32),
                pltpu.VMEM((2, n_all, 8, chunk), f32),
                pltpu.VMEM((2, n_all, 8, chunk), f32),
                pltpu.VMEM((reach, piece, LANES), f32),
                pltpu.VMEM((reach, piece, LANES), f32),
                pltpu.VMEM((1, rows), f32),
                pltpu.VMEM((feats, 2, 1, rows), f32),
                pltpu.VMEM((reach, 1, piece), f32),
                pltpu.VMEM((reach, feats, 1, piece), f32),
                dma((2,)),
                dma((feats, n_all)),
                dma((feats, n_all)),
                dma((reach, feats, n_key)),
                dma((reach, feats, n_key)),
                dma((feats, n_all)),
                dma((feats, n_all)),
                dma((2 + reach,)),
                dma((2 + reach,)),
                dma((feats, 2)),
                dma((feats, 2)),
                dma((reach, feats)),
                dma((reach, feats)),
            ],
            compiler_params=pltpu.CompilerParams(
                collective_id=0, has_side_effects=True, vmem_limit_bytes=63 * 1024 * 1024
            ),
            name="chamfer",
        )(frames, clip_label.reshape(1, rows))
        return out.reshape(rows)

    in_specs = (P(("groups", "blk", "sub"), "feat"), P(("groups", "blk", "sub")))
    out_specs = P(("groups", "blk", "sub"))
    return jax.shard_map(body, mesh=mesh, in_specs=in_specs, out_specs=out_specs, check_vma=False)
```
